1024 devices in a mesh: dp: 16 (over x, y), expert: 64 (over z, core).
Axes of the slice: x: 4, y: 4, z: 32, core: 2. Of those that a mesh axis runs over, the one named last changes fastest.
Arguments:
- tokens: bfloat16 [131072, 2048], P(('dp', 'expert')), may hold values from -6 to 6
- expert_ids: int32 [131072], P(('dp', 'expert')), may hold values from 0 to 63
- gate: float32 [131072], P(('dp', 'expert')), may hold values from 0.2 to 1
- cotangent: bfloat16 [131072, 2048], P(('dp', 'expert')), may hold values from -6 to 6
- w_up: bfloat16 [64, 2048, 768], P('expert'), may hold values from -0.125 to 0.125
- w_down: bfloat16 [64, 768, 2048], P('expert'), may hold values from -0.21875 to 0.21875
Outputs:
- layer_out: bfloat16 [131072, 2048], P(('dp', 'expert'))
- token_grad: bfloat16 [131072, 2048], P(('dp', 'expert'))
- up_grad: float32 [64, 2048, 768], P('expert', 'dp')
- down_grad: float32 [64, 768, 2048], P('expert', None, 'dp')
The draws below stay inside these ranges and needn't reach their ends.
All inputs are finite; a program needn't handle non-finite values.
Results may differ from the reference program's by a relative error of at most 0.013.
Values may be sent and summed in bfloat16 or wider, within the bound.
No kernel may reach another device: no remote copies, remote signals or barrier semaphores. Data moves between devices by JAX's collectives and lax.ppermute only.
A program may use at most 64 MiB of HBM per device.

```python
import math
import jax
import jax.numpy as jnp
import numpy as np
from jax import lax

D = 2048
FF = 768
TOK_DEV = 128
EXPERTS = 64
CAPACITY = 2
TOKENS = 131072
N_DP = 16
N_EXPERT = 64


def set_ends(entries, rng, least, top_value):
    shape = entries.shape
    index_at = [jax.random.randint(jax.random.fold_in(rng, axis), (), 0, shape[axis]) for axis in range(len(shape))]
    entries = entries.at[tuple(index_at)].set(least)
    longest = shape.index(max(shape))
    index_at[longest] = (index_at[longest] + 1) % shape[longest]
    return entries.at[tuple(index_at)].set(top_value)


def levels(rng, shape, shards, least, high):
    level = 1.0
    for dim, shards_of in shards:
        draws = jax.random.uniform(jax.random.fold_in(jax.random.fold_in(rng, 6), dim), (shards_of,), jnp.float32, least / len(shards), high / len(shards))
        level = level * jnp.repeat(jnp.exp(draws), shape[dim] // shards_of).reshape((-1,) + (1,) * (len(shape) - 1 - dim))
    return level


def rank_bounds(count, lean):
    portions = [(1 << 20) // math.isqrt(rank ** lean) + 1 for rank in range(1, count + 1)]
    deviation = 1 + sum(portions) // (1 << 30)
    return np.cumsum(np.array([max(1, weight // deviation) for weight in portions]))


def ranked_ids(own_key, shape, amount, skew):
    grid = rank_bounds(amount, skew)
    lot = jax.random.randint(jax.random.fold_in(own_key, 1), shape, 0, int(grid[amount - 1]))
    rank = jnp.searchsorted(jnp.asarray(grid, jnp.int32), lot, side="right")
    return jax.random.permutation(jax.random.fold_in(own_key, 2), amount)[rank].astype(jnp.int32)


def bell_draw(rng, dims, width, most, shards=(), kind=jnp.bfloat16):
    entries = width * jax.random.normal(rng, dims, jnp.float32)
    if shards:
        entries = entries * levels(rng, dims, shards, -0.22, 0.18)
    return jnp.clip(entries, -most, most).astype(kind)


def setup_inputs(seed: int = 0) -> dict:
    key_list = jax.random.split(jax.random.key(seed), 7)
    return {
        "tokens": bell_draw(key_list[0], (TOKENS, D), 1.0, 6.0, ((0, 1024),)),
        "expert_ids": set_ends(ranked_ids(key_list[1], (TOKENS,), EXPERTS, 2), jax.random.fold_in(key_list[1], 3), 0, EXPERTS - 1).astype(jnp.int32),
        "gate": jnp.clip(0.2 + 0.8 * jax.random.uniform(key_list[2], (TOKENS,), jnp.float32) ** levels(key_list[2], (TOKENS,), ((0, 1024),), -0.2, 0.2), 0.2, 1.0),
        "cotangent": bell_draw(key_list[3], (TOKENS, D), 1.0, 6.0, ((0, 1024),)),
        "w_up": bell_draw(key_list[4], (EXPERTS, D, FF), D ** -0.5, 0.125, ((0, 64),)),
        "w_down": bell_draw(key_list[5], (EXPERTS, FF, D), FF ** -0.5, 0.21875, ((0, 64),)),
    }


def reference(tokens, expert_ids, gate, cotangent, w_up, w_down):
    block_count = N_DP * N_EXPERT
    id_blocks = expert_ids.reshape(block_count, TOK_DEV)
    onehot = (id_blocks[:, :, None] == jnp.arange(EXPERTS, dtype=jnp.int32)[None, None, :]).astype(jnp.int32)
    row_rank = jnp.sum((jnp.cumsum(onehot, axis=1) - onehot) * onehot, axis=2)
    kept = row_rank < CAPACITY
    source = (jnp.arange(block_count, dtype=jnp.int32) % N_EXPERT)[:, None]
    per_expert = N_EXPERT * CAPACITY
    slot_total = EXPERTS * per_expert
    target = jnp.where(kept, id_blocks * per_expert + source * CAPACITY + row_rank, slot_total).astype(jnp.int32)
    scaled = (gate[:, None] * cotangent.astype(jnp.float32)).astype(jnp.bfloat16)
    group_rows = N_EXPERT * TOK_DEV
    w_in = w_up.astype(jnp.float32)
    w_out = w_down.astype(jnp.float32)

    def one_group(totals, inputs):
        group_tokens, group_scaled, group_target = inputs
        live = group_target < slot_total
        slot_x = jnp.zeros((slot_total, D), jnp.bfloat16).at[group_target].set(group_tokens, mode="drop")
        slot_c = jnp.zeros((slot_total, D), jnp.bfloat16).at[group_target].set(group_scaled, mode="drop")
        slot_x = slot_x.reshape(EXPERTS, per_expert, D).astype(jnp.float32)
        slot_c = slot_c.reshape(EXPERTS, per_expert, D).astype(jnp.float32)
        pre_act = jnp.einsum("erd,edf->erf", slot_x, w_in)
        hidden = jax.nn.silu(pre_act).astype(jnp.bfloat16)
        expert_out = jnp.einsum("erf,efd->erd", hidden.astype(jnp.float32), w_out).astype(jnp.bfloat16)
        back = jnp.einsum("erd,efd->erf", slot_c, w_out)
        sigma = jax.nn.sigmoid(pre_act)
        grad_pre = (back * sigma * (1.0 + pre_act * (1.0 - sigma))).astype(jnp.bfloat16)
        slot_grad = jnp.einsum("erf,edf->erd", grad_pre.astype(jnp.float32), w_in).astype(jnp.bfloat16)
        up_part = jnp.einsum("erd,erf->edf", slot_x, grad_pre.astype(jnp.float32)).astype(jnp.bfloat16)
        down_part = jnp.einsum("erf,erd->efd", hidden.astype(jnp.float32), slot_c).astype(jnp.bfloat16)
        index = jnp.minimum(group_target, slot_total - 1)
        out_rows = jnp.take(expert_out.reshape(slot_total, D), index, axis=0)
        grad_rows = jnp.take(slot_grad.reshape(slot_total, D), index, axis=0)
        out_rows = jnp.where(live[:, None], out_rows, jnp.zeros_like(out_rows))
        grad_rows = jnp.where(live[:, None], grad_rows, jnp.zeros_like(grad_rows))
        totals = (totals[0] + up_part.astype(jnp.float32), totals[1] + down_part.astype(jnp.float32))
        return totals, (out_rows, grad_rows)

    start = (jnp.zeros((EXPERTS, D, FF), jnp.float32), jnp.zeros((EXPERTS, FF, D), jnp.float32))
    inputs = (tokens.reshape(N_DP, group_rows, D), scaled.reshape(N_DP, group_rows, D), target.reshape(N_DP, group_rows))
    totals, rows = lax.scan(one_group, start, inputs)
    expert_out = rows[0].reshape(TOKENS, D)
    token_grad = rows[1].reshape(TOKENS, D)
    layer_out = (gate[:, None] * expert_out.astype(jnp.float32)).astype(jnp.bfloat16)
    inverse = 1.0 / N_DP
    return layer_out, token_grad, totals[0] * inverse, totals[1] * inverse
```

```python
import jax
import jax.numpy as jnp
from jax import lax
from jax.experimental import pallas as pl
from jax.experimental.pallas import tpu as pltpu
from jax.sharding import PartitionSpec as P


F32 = jnp.float32
BF16 = jnp.bfloat16
I32 = jnp.int32
VMEM_LIMIT = 56 * 1024 * 1024


def iota(shape, dim):
    return lax.broadcasted_iota(I32, shape, dim)


def row_base(ids_row):
    n = ids_row.shape[1]
    ids = jnp.broadcast_to(ids_row.astype(F32), (n, n))
    same = ids == ids.T
    earlier = iota((n, n), 0) < iota((n, n), 1)
    rank = jnp.sum(jnp.where(same & earlier, 1.0, 0.0), axis=0, keepdims=True)
    return jnp.where(rank < 2.0, 8.0 * ids_row.astype(F32) + rank, -1024.0)


def column(row):
    n = row.shape[1]
    return jnp.broadcast_to(row, (n, n)).T


def one_hot(mask):
    return jnp.where(mask, 1.0, 0.0).astype(BF16)


def dispatch_kernel(ids_ref, gate_ref, tok_ref, cot_ref, send_ref, sel, src):
    n, width = tok_ref.shape
    half = width // 2
    base = row_base(ids_ref[...]).astype(I32)
    rows = iota((4 * n, n), 0)
    gate = column(gate_ref[...])[:, :1]
    for h in range(2):
        cols = pl.ds(h * half, half)
        src[pl.ds(h * n, n), :] = tok_ref[:, cols]
        src[pl.ds((2 + h) * n, n), :] = (gate * cot_ref[:, cols].astype(F32)).astype(BF16)
    for b in range(4):
        sel[:, pl.ds(b * n, n)] = one_hot(rows == base + 2 * b)
    send_ref[...] = jnp.dot(sel[...], src[...], preferred_element_type=F32).astype(BF16)


def dispatch(ids, gate, tokens, cotangent):
    n, width = tokens.shape
    return pl.pallas_call(
        dispatch_kernel,
        out_shape=jax.ShapeDtypeStruct((4 * n, width // 2), BF16),
        scratch_shapes=[pltpu.VMEM((4 * n, 4 * n), BF16), pltpu.VMEM((4 * n, width // 2), BF16)],
        compiler_params=pltpu.CompilerParams(vmem_limit_bytes=VMEM_LIMIT),
        name="dispatch",
    )(ids, gate, tokens, cotangent)


def dot_t(a, b):
    return lax.dot_general(a, b, (((1,), (1,)), ((), ())), preferred_element_type=F32)


def expert_kernel(arr_ref, wu_ref, wd_ref, send_ref, x_ref, c_ref, hid_ref, gp_ref, perm, rows):
    m, half = arr_ref.shape
    n = m // 4
    t = iota((n, m), 0)
    at = (t // 2) * 8 + t % 2
    for b in range(4):
        perm[pl.ds(b * n, n), :] = one_hot(iota((n, m), 1) == at + 2 * b)
    rows[...] = jnp.dot(perm[...], arr_ref[...], preferred_element_type=F32).astype(BF16)
    pre = jnp.zeros((n, wu_ref.shape[1]), F32)
    back = jnp.zeros((n, wu_ref.shape[1]), F32)
    for h in range(2):
        cols = pl.ds(h * half, half)
        x = rows[pl.ds(h * n, n), :]
        c = rows[pl.ds((2 + h) * n, n), :]
        x_ref[:, cols] = x
        c_ref[:, cols] = c
        pre += jnp.dot(x, wu_ref[cols, :], preferred_element_type=F32)
        back += dot_t(c, wd_ref[:, cols])
    sigma = 1.0 / (1.0 + jnp.exp(-pre))
    hidden = (pre * sigma).astype(BF16)
    grad = (back * sigma * (1.0 + pre * (1.0 - sigma))).astype(BF16)
    hid_ref[...] = hidden
    gp_ref[...] = grad
    for h in range(2):
        cols = pl.ds(h * half, half)
        rows[pl.ds(h * n, n), :] = jnp.dot(hidden, wd_ref[:, cols], preferred_element_type=F32).astype(BF16)
        rows[pl.ds((2 + h) * n, n), :] = dot_t(grad, wu_ref[cols, :]).astype(BF16)
    send_ref[...] = lax.dot_general(
        perm[...], rows[...], (((0,), (0,)), ((), ())), preferred_element_type=F32
    ).astype(BF16)


def expert(arrived, w_up, w_down):
    m, half = arrived.shape
    n, width, ff = m // 4, 2 * half, w_up.shape[1]
    shape = jax.ShapeDtypeStruct
    return pl.pallas_call(
        expert_kernel,
        out_shape=(
            shape((m, half), BF16),
            shape((n, width), BF16),
            shape((n, width), BF16),
            shape((n, ff), BF16),
            shape((n, ff), BF16),
        ),
        scratch_shapes=[pltpu.VMEM((m, m), BF16), pltpu.VMEM((m, half), BF16)],
        compiler_params=pltpu.CompilerParams(vmem_limit_bytes=VMEM_LIMIT),
        name="expert",
    )(arrived, w_up, w_down)


def combine_kernel(ids_ref, gate_ref, arr_ref, out_ref, grad_ref, sel):
    n, width = out_ref.shape
    half = width // 2
    base = column(row_base(ids_ref[...])).astype(I32)[:, :1]
    gate = column(gate_ref[...])[:, :1]
    cols = iota((n, 4 * n), 1)
    for b in range(4):
        sel[pl.ds(b * n, n), :] = one_hot(cols == base + 2 * b)
    for h in range(2):
        o = jnp.dot(sel[pl.ds(h * n, n), :], arr_ref[...], preferred_element_type=F32)
        g = jnp.dot(sel[pl.ds((2 + h) * n, n), :], arr_ref[...], preferred_element_type=F32)
        out_ref[:, pl.ds(h * half, half)] = (gate * o).astype(BF16)
        grad_ref[:, pl.ds(h * half, half)] = g.astype(BF16)


def combine(ids, gate, arrived, n, width):
    shape = jax.ShapeDtypeStruct((n, width), BF16)
    return pl.pallas_call(
        combine_kernel,
        out_shape=(shape, shape),
        scratch_shapes=[pltpu.VMEM((4 * n, 4 * n), BF16)],
        compiler_params=pltpu.CompilerParams(vmem_limit_bytes=VMEM_LIMIT),
        name="combine",
    )(ids, gate, arrived)


def wgrad_kernel(where_ref, x_ref, c_ref, hid_ref, gp_ref, up_ref, down_ref):
    numbers = (((0,), (0,)), ((), ()))
    up_ref[0] = lax.dot_general(x_ref[...], gp_ref[...], numbers, preferred_element_type=F32).astype(BF16)
    down_ref[0] = lax.dot_general(hid_ref[...], c_ref[...], numbers, preferred_element_type=F32).astype(BF16)


def wgrad(where, rows_x, rows_c, hidden, grad, side):
    n, width = rows_x.shape
    ff = hidden.shape[1]
    parts = side * side
    block = width // parts

    def x_at(i, where):
        return 0, ((where[0] + i // side) % side) * side + (where[1] + i % side) % side

    def c_at(i, where):
        return 0, ((where[0] + i % side) % side) * side + (where[1] + i // side) % side

    whole = lambda i, where: (0, 0)
    at = lambda i, where: (i, 0, 0)
    return pl.pallas_call(
        wgrad_kernel,
        grid_spec=pltpu.PrefetchScalarGridSpec(
            num_scalar_prefetch=1,
            grid=(parts,),
            in_specs=[
                pl.BlockSpec((n, block), x_at),
                pl.BlockSpec((n, block), c_at),
                pl.BlockSpec((n, ff), whole),
                pl.BlockSpec((n, ff), whole),
            ],
            out_specs=[pl.BlockSpec((1, block, ff), at), pl.BlockSpec((1, ff, block), at)],
        ),
        out_shape=(
            jax.ShapeDtypeStruct((parts, block, ff), BF16),
            jax.ShapeDtypeStruct((parts, ff, block), BF16),
        ),
        cost_estimate=pl.CostEstimate(
            flops=4 * n * width * ff, bytes_accessed=4 * width * ff + 4 * n * (width + ff), transcendentals=0
        ),
        name="wgrad",
    )(where, rows_x, rows_c, hidden, grad)


def ring_scatter(a, axis, side, last):
    def send(v, step):
        pairs = []
        for px in range(side):
            for py in range(side):
                tx, ty = ((px + step) % side, py) if axis == "x" else (px, (py + step) % side)
                pairs.append((px * side + py, tx * side + ty))
        return lax.ppermute(v, "dp", pairs)

    half = a.shape[1] // 2
    add = lambda p, q: (p.astype(F32) + q.astype(F32)).astype(BF16)
    ahead = send(a[2, :half], 1)
    behind = send(a[2, half:], -1)
    ahead = send(jnp.concatenate([add(a[1, :half], ahead), a[1, half:]], 0), 1)
    behind = send(jnp.concatenate([a[3, :half], add(a[3, half:], behind)], 0), -1)
    total = a[0].astype(F32) + ahead.astype(F32) + behind.astype(F32)
    return total * (1.0 / (side * side)) if last else total.astype(BF16)


def scatter(parts, order, side):
    count, rows, cols = parts.shape
    first = ring_scatter(parts.reshape(side, side * rows, cols), order[0], side, False)
    return ring_scatter(first.reshape(side, rows, cols), order[1], side, True)


def shards(tokens, expert_ids, gate, cotangent, w_up, w_down):
    n, width = tokens.shape
    experts = lax.axis_size("expert")
    side = 4
    ids = expert_ids.reshape(1, n)
    gates = gate.reshape(1, n)

    def exchange(v):
        v = v.reshape(experts, -1, v.shape[1])
        v = lax.all_to_all(v, "expert", split_axis=0, concat_axis=0, tiled=True)
        return v.reshape(-1, v.shape[2])

    arrived = exchange(dispatch(ids, gates, tokens, cotangent))
    send, rows_x, rows_c, hidden, grad = expert(arrived, w_up[0], w_down[0])
    returned = exchange(send)
    place = lax.axis_index("dp")
    where = jnp.stack([place // side, place % side]).astype(I32)
    up, down = wgrad(where, rows_x, rows_c, hidden, grad, side)
    up = scatter(up, "xy", side)
    down = scatter(down, "yx", side)
    layer_out, token_grad = combine(ids, gates, returned, n, width)
    return layer_out, token_grad, up[None], down[None]


def solution(mesh):
    in_specs = (
        P(("dp", "expert"), None),
        P(("dp", "expert")),
        P(("dp", "expert")),
        P(("dp", "expert"), None),
        P("expert", None, None),
        P("expert", None, None),
    )
    out_specs = (
        P(("dp", "expert"), None),
        P(("dp", "expert"), None),
        P("expert", "dp", None),
        P("expert", None, "dp"),
    )
    return jax.shard_map(shards, mesh=mesh, in_specs=in_specs, out_specs=out_specs, check_vma=False)
```

```python
import jax
import jax.numpy as jnp
from jax import lax
from jax.experimental import pallas as pl
from jax.experimental.pallas import tpu as pltpu
from jax.sharding import PartitionSpec as P


F32 = jnp.float32
BF16 = jnp.bfloat16
I32 = jnp.int32
VMEM_LIMIT = 60 * 1024 * 1024
ON_CHIP = pl.BlockSpec(memory_space=pltpu.VMEM)
IN_HBM = pl.BlockSpec(memory_space=pltpu.HBM)


def iota(shape, dim):
    return lax.broadcasted_iota(I32, shape, dim)


def row_base(ids_row, place_ref):
    n = ids_row.shape[1]
    experts = place_ref.shape[0]
    mine = iota((experts, n), 0) == ids_row
    place = jnp.sum(jnp.where(mine, place_ref[...], 0.0), axis=0, keepdims=True)
    ids = jnp.broadcast_to(ids_row.astype(F32), (n, n))
    same = ids == ids.T
    earlier = iota((n, n), 0) < iota((n, n), 1)
    rank = jnp.sum(jnp.where(same & earlier, 1.0, 0.0), axis=0, keepdims=True)
    return jnp.where(rank < 2.0, 8.0 * place + rank, -1024.0)


def column(row):
    n = row.shape[1]
    return jnp.broadcast_to(row, (n, n)).T


def one_hot(mask):
    return jnp.where(mask, 1.0, 0.0).astype(BF16)


def dispatch_kernel(ids_ref, place_ref, gate_ref, tok_ref, cot_ref, send_ref, sel, src, cot, sem):
    n, width = tok_ref.shape
    half = width // 2
    cot_copy = pltpu.make_async_copy(cot_ref, cot, sem.at[2])
    cot_copy.start()
    tok_copies = []
    for h in range(2):
        copy = pltpu.make_async_copy(tok_ref.at[:, pl.ds(h * half, half)], src.at[pl.ds(h * n, n), :], sem.at[h])
        copy.start()
        tok_copies.append(copy)
    base = row_base(ids_ref[...], place_ref).astype(I32)
    rows = iota((4 * n, n), 0)
    gate = column(gate_ref[...])[:, :1]
    for b in range(4):
        sel[:, pl.ds(b * n, n)] = one_hot(rows == base + 2 * b)
    cot_copy.wait()
    for h in range(2):
        c = cot[:, pl.ds(h * half, half)].astype(F32)
        src[pl.ds((2 + h) * n, n), :] = (gate * c).astype(BF16)
    for copy in tok_copies:
        copy.wait()
    send_ref[...] = jnp.dot(sel[...], src[...], preferred_element_type=F32).astype(BF16)


def dispatch(ids, place, gate, tokens, cotangent):
    n, width = tokens.shape
    return pl.pallas_call(
        dispatch_kernel,
        out_shape=jax.ShapeDtypeStruct((4 * n, width // 2), BF16),
        in_specs=[ON_CHIP] * 3 + [IN_HBM] * 2,
        out_specs=ON_CHIP,
        scratch_shapes=[
            pltpu.VMEM((4 * n, 4 * n), BF16),
            pltpu.VMEM((4 * n, width // 2), BF16),
            pltpu.VMEM((n, width), BF16),
            pltpu.SemaphoreType.DMA((3,)),
        ],
        compiler_params=pltpu.CompilerParams(vmem_limit_bytes=VMEM_LIMIT),
        name="dispatch",
    )(ids, place, gate, tokens, cotangent)


def dot_t(a, b):
    return lax.dot_general(a, b, (((1,), (1,)), ((), ())), preferred_element_type=F32)


def expert_kernel(
    arr_hbm, wu_hbm, wd_hbm, send_hbm, x_hbm, c_hbm, hid_hbm, gp_hbm,
    arr_ref, wu_ref, wd_ref, send_ref, perm, rows, back_rows, hid, gp, load_sem, store_sem,
):
    m, half = arr_ref.shape
    n = m // 4
    part = n // 2
    block = m // 2
    halves = [pl.ds(a * block, block) for a in range(2)]
    loads = [(arr_hbm.at[here, :], arr_ref.at[here, :]) for here in halves]
    loads += [(wu_hbm.at[pl.ds(h * half, half), :], wu_ref.at[pl.ds(h * half, half), :]) for h in range(2)]
    loads += [(wd_hbm, wd_ref)]
    loads = [pltpu.make_async_copy(src, dst, load_sem.at[i]) for i, (src, dst) in enumerate(loads)]
    for copy in loads:
        copy.start()
    t = iota((part, block), 0)
    at = (t // 2) * 8 + t % 2
    for b in range(4):
        perm[pl.ds(b * part, part), :] = one_hot(iota((part, block), 1) == at + 2 * b)
    for a in range(2):
        loads[a].wait()
        moved = jnp.dot(perm[...], arr_ref[pl.ds(a * block, block), :], preferred_element_type=F32).astype(BF16)
        for b in range(4):
            rows[pl.ds(b * n + a * part, part), :] = moved[b * part : (b + 1) * part]
    stores = []

    def store(src, dst):
        copy = pltpu.make_async_copy(src, dst, store_sem.at[len(stores)])
        copy.start()
        stores.append(copy)

    for h in range(2):
        cols = pl.ds(h * half, half)
        store(rows.at[pl.ds(h * n, n), :], x_hbm.at[:, cols])
        store(rows.at[pl.ds((2 + h) * n, n), :], c_hbm.at[:, cols])
    pre = jnp.zeros((n, wu_ref.shape[1]), F32)
    for h in range(2):
        loads[2 + h].wait()
        pre += jnp.dot(rows[pl.ds(h * n, n), :], wu_ref[pl.ds(h * half, half), :], preferred_element_type=F32)
    sigma = 1.0 / (1.0 + jnp.exp(-pre))
    hidden = (pre * sigma).astype(BF16)
    hid[...] = hidden
    store(hid, hid_hbm)
    loads[4].wait()
    back = jnp.zeros((n, wu_ref.shape[1]), F32)
    for h in range(2):
        back += dot_t(rows[pl.ds((2 + h) * n, n), :], wd_ref[:, pl.ds(h * half, half)])
    grad = (back * sigma * (1.0 + pre * (1.0 - sigma))).astype(BF16)
    gp[...] = grad
    store(gp, gp_hbm)
    for h in range(2):
        cols = pl.ds(h * half, half)
        out = jnp.dot(hidden, wd_ref[:, cols], preferred_element_type=F32).astype(BF16)
        xgrad = dot_t(grad, wu_ref[cols, :]).astype(BF16)
        for a in range(2):
            took = slice(a * part, (a + 1) * part)
            back_rows[pl.ds(a * block + h * part, part), :] = out[took]
            back_rows[pl.ds(a * block + (2 + h) * part, part), :] = xgrad[took]
    for a in range(2):
        here = pl.ds(a * block, block)
        send_ref[here, :] = lax.dot_general(
            perm[...], back_rows[here, :], (((0,), (0,)), ((), ())), preferred_element_type=F32
        ).astype(BF16)
        store(send_ref.at[here, :], send_hbm.at[here, :])
    for copy in stores:
        copy.wait()


def expert(arrived, w_up, w_down):
    m, half = arrived.shape
    n, width, ff = m // 4, 2 * half, w_up.shape[1]
    shape = jax.ShapeDtypeStruct
    return pl.pallas_call(
        expert_kernel,
        out_shape=(
            shape((m, half), BF16),
            shape((n, width), BF16),
            shape((n, width), BF16),
            shape((n, ff), BF16),
            shape((n, ff), BF16),
        ),
        in_specs=[IN_HBM] * 3,
        out_specs=[IN_HBM] * 5,
        scratch_shapes=[
            pltpu.VMEM((m, half), BF16),
            pltpu.VMEM((width, ff), BF16),
            pltpu.VMEM((ff, width), BF16),
            pltpu.VMEM((m, half), BF16),
            pltpu.VMEM((m // 2, m // 2), BF16),
            pltpu.VMEM((m, half), BF16),
            pltpu.VMEM((m, half), BF16),
            pltpu.VMEM((n, ff), BF16),
            pltpu.VMEM((n, ff), BF16),
            pltpu.SemaphoreType.DMA((5,)),
            pltpu.SemaphoreType.DMA((8,)),
        ],
        compiler_params=pltpu.CompilerParams(vmem_limit_bytes=VMEM_LIMIT),
        name="expert",
    )(arrived, w_up, w_down)


def plan_kernel(ids_ref, place_ref, after_ref, sel):
    m = sel.shape[0]
    n = m // 4
    base = column(row_base(ids_ref[...], place_ref)).astype(I32)[:, :1]
    cols = iota((n, m), 1)
    for b in range(4):
        sel[pl.ds(b * n, n), :] = one_hot(cols == base + 2 * b)


def plan(ids, place, after):
    m = 4 * ids.shape[1]
    return pl.pallas_call(
        plan_kernel,
        out_shape=jax.ShapeDtypeStruct((m, m), BF16),
        in_specs=[ON_CHIP, ON_CHIP, IN_HBM],
        out_specs=ON_CHIP,
        name="plan",
    )(ids, place, after)


def combine_kernel(sel_ref, gate_ref, arr_ref, out_ref, grad_ref):
    n = out_ref.shape[0]
    h = pl.program_id(0)
    gate = column(gate_ref[...])[:, :1]
    o = jnp.dot(sel_ref[pl.ds(h * n, n), :], arr_ref[...], preferred_element_type=F32)
    g = jnp.dot(sel_ref[pl.ds((2 + h) * n, n), :], arr_ref[...], preferred_element_type=F32)
    out_ref[...] = (gate * o).astype(BF16)
    grad_ref[...] = g.astype(BF16)


def combine(sel, gate, arrived, n, width):
    shape = jax.ShapeDtypeStruct((n, width), BF16)
    block = pl.BlockSpec((n, width // 2), lambda h: (0, h))
    return pl.pallas_call(
        combine_kernel,
        out_shape=(shape, shape),
        grid=(2,),
        in_specs=[ON_CHIP] * 3,
        out_specs=[block, block],
        compiler_params=pltpu.CompilerParams(vmem_limit_bytes=VMEM_LIMIT // 3),
        name="combine",
    )(sel, gate, arrived)


def wgrad_kernel(where_ref, x_ref, c_ref, hid_ref, gp_ref, up_ref, down_ref):
    numbers = (((0,), (0,)), ((), ()))
    up_ref[0] = lax.dot_general(x_ref[...], gp_ref[...], numbers, preferred_element_type=F32).astype(BF16)
    down_ref[0] = lax.dot_general(hid_ref[...], c_ref[...], numbers, preferred_element_type=F32).astype(BF16)


def wgrad(where, rows_x, rows_c, hidden, grad, side):
    n, width = rows_x.shape
    ff = hidden.shape[1]
    parts = side * side
    block = width // parts

    def x_at(i, where):
        return 0, ((where[0] + i // side) % side) * side + (where[1] + i % side) % side

    def c_at(i, where):
        return 0, ((where[0] + i % side) % side) * side + (where[1] + i // side) % side

    whole = lambda i, where: (0, 0)
    at = lambda i, where: (i, 0, 0)
    return pl.pallas_call(
        wgrad_kernel,
        grid_spec=pltpu.PrefetchScalarGridSpec(
            num_scalar_prefetch=1,
            grid=(parts,),
            in_specs=[
                pl.BlockSpec((n, block), x_at),
                pl.BlockSpec((n, block), c_at),
                pl.BlockSpec((n, ff), whole),
                pl.BlockSpec((n, ff), whole),
            ],
            out_specs=[pl.BlockSpec((1, block, ff), at), pl.BlockSpec((1, ff, block), at)],
        ),
        out_shape=(
            jax.ShapeDtypeStruct((parts, block, ff), BF16),
            jax.ShapeDtypeStruct((parts, ff, block), BF16),
        ),
        cost_estimate=pl.CostEstimate(
            flops=4 * n * width * ff, bytes_accessed=4 * width * ff + 4 * n * (width + ff), transcendentals=0
        ),
        name="wgrad",
    )(where, rows_x, rows_c, hidden, grad)


def ring_scatter(a, axis, side, last):
    def send(v, step):
        pairs = []
        for px in range(side):
            for py in range(side):
                tx, ty = ((px + step) % side, py) if axis == "x" else (px, (py + step) % side)
                pairs.append((px * side + py, tx * side + ty))
        return lax.ppermute(v, "dp", pairs)

    half = a.shape[1] // 2
    add = lambda p, q: (p.astype(F32) + q.astype(F32)).astype(BF16)
    ahead = send(a[2, :half], 1)
    behind = send(a[2, half:], -1)
    ahead = send(jnp.concatenate([add(a[1, :half], ahead), a[1, half:]], 0), 1)
    behind = send(jnp.concatenate([a[3, :half], add(a[3, half:], behind)], 0), -1)
    total = a[0].astype(F32) + ahead.astype(F32) + behind.astype(F32)
    return total * (1.0 / (side * side)) if last else total.astype(BF16)


def scatter(parts, order, side):
    count, rows, cols = parts.shape
    first = ring_scatter(parts.reshape(side, side * rows, cols), order[0], side, False)
    return ring_scatter(first.reshape(side, rows, cols), order[1], side, True)


CHIP_ORDER = (19, 6, 9, 20, 24, 22, 27, 1, 10, 28, 3, 13, 2, 5, 18, 25,
              23, 17, 7, 14, 31, 15, 26, 0, 12, 4, 11, 29, 16, 21, 8, 30)


def exchange_order(experts):
    return [2 * chip + core for chip in CHIP_ORDER for core in range(2)]


def shards(tokens, expert_ids, gate, cotangent, w_up, w_down):
    n, width = tokens.shape
    experts = lax.axis_size("expert")
    order = exchange_order(experts)
    side = 4
    ids = expert_ids.reshape(1, n)
    gates = gate.reshape(1, n)

    def exchange(v):
        v = v.reshape(experts, -1, v.shape[1])
        v = lax.all_to_all(
            v, "expert", split_axis=0, concat_axis=0, tiled=True, axis_index_groups=[order]
        )
        return v.reshape(-1, v.shape[2])

    place = [0] * experts
    for at, e in enumerate(order):
        place[e] = at
    place = jnp.broadcast_to(jnp.asarray(place, F32)[:, None], (experts, n))
    arrived = exchange(dispatch(ids, place, gates, tokens, cotangent))
    send, rows_x, rows_c, hidden, grad = expert(arrived, w_up[0], w_down[0])
    returned = exchange(send)
    here = lax.axis_index("dp")
    where = jnp.stack([here // side, here % side]).astype(I32)
    up, down = wgrad(where, rows_x, rows_c, hidden, grad, side)
    up = scatter(up, "xy", side)
    down = scatter(down, "yx", side)
    layer_out, token_grad = combine(plan(ids, place, grad), gates, returned, n, width)
    return layer_out, token_grad, up[None], down[None]


def solution(mesh):
    in_specs = (
        P(("dp", "expert"), None),
        P(("dp", "expert")),
        P(("dp", "expert")),
        P(("dp", "expert"), None),
        P("expert", None, None),
        P("expert", None, None),
    )
    out_specs = (
        P(("dp", "expert"), None),
        P(("dp", "expert"), None),
        P("expert", "dp", None),
        P("expert", None, "dp"),
    )
    return jax.shard_map(shards, mesh=mesh, in_specs=in_specs, out_specs=out_specs, check_vma=False)
```

```python
import functools

import jax
import jax.numpy as jnp
import numpy as np
from jax import lax
from jax.experimental import pallas as pl
from jax.experimental.pallas import tpu as pltpu
from jax.sharding import PartitionSpec as P


F32 = jnp.float32
BF16 = jnp.bfloat16
I32 = jnp.int32
VMEM_LIMIT = 60 * 1024 * 1024
ON_CHIP = pl.BlockSpec(memory_space=pltpu.VMEM)
IN_HBM = pl.BlockSpec(memory_space=pltpu.HBM)


def iota(shape, dim):
    return lax.broadcasted_iota(I32, shape, dim)


def row_base(ids_row, place_ref):
    n = ids_row.shape[1]
    experts = place_ref.shape[0]
    mine = iota((experts, n), 0) == ids_row
    place = jnp.sum(jnp.where(mine, place_ref[...], 0.0), axis=0, keepdims=True)
    ids = jnp.broadcast_to(ids_row.astype(F32), (n, n))
    same = ids == ids.T
    earlier = iota((n, n), 0) < iota((n, n), 1)
    rank = jnp.sum(jnp.where(same & earlier, 1.0, 0.0), axis=0, keepdims=True)
    return jnp.where(rank < 2.0, 8.0 * place + rank, -1024.0)


def column(row):
    n = row.shape[1]
    return jnp.broadcast_to(row, (n, n)).T


def one_hot(mask):
    return jnp.where(mask, 1.0, 0.0).astype(BF16)


def dispatch_kernel(ids_ref, place_ref, gate_ref, tok_ref, cot_ref, send_ref, sel, src, cot, sem):
    n, width = tok_ref.shape
    half = width // 2
    cot_copy = pltpu.make_async_copy(cot_ref, cot, sem.at[2])
    cot_copy.start()
    tok_copies = []
    for h in range(2):
        copy = pltpu.make_async_copy(tok_ref.at[:, pl.ds(h * half, half)], src.at[pl.ds(h * n, n), :], sem.at[h])
        copy.start()
        tok_copies.append(copy)
    base = row_base(ids_ref[...], place_ref).astype(I32)
    rows = iota((4 * n, n), 0)
    gate = column(gate_ref[...])[:, :1]
    for b in range(4):
        sel[:, pl.ds(b * n, n)] = one_hot(rows == base + 2 * b)
    cot_copy.wait()
    for h in range(2):
        c = cot[:, pl.ds(h * half, half)].astype(F32)
        src[pl.ds((2 + h) * n, n), :] = (gate * c).astype(BF16)
    for copy in tok_copies:
        copy.wait()
    send_ref[...] = jnp.dot(sel[...], src[...], preferred_element_type=F32).astype(BF16)


def dispatch(ids, place, gate, tokens, cotangent):
    n, width = tokens.shape
    return pl.pallas_call(
        dispatch_kernel,
        out_shape=jax.ShapeDtypeStruct((4 * n, width // 2), BF16),
        in_specs=[ON_CHIP] * 3 + [IN_HBM] * 2,
        out_specs=ON_CHIP,
        scratch_shapes=[
            pltpu.VMEM((4 * n, 4 * n), BF16),
            pltpu.VMEM((4 * n, width // 2), BF16),
            pltpu.VMEM((n, width), BF16),
            pltpu.SemaphoreType.DMA((3,)),
        ],
        compiler_params=pltpu.CompilerParams(vmem_limit_bytes=VMEM_LIMIT),
        name="dispatch",
    )(ids, place, gate, tokens, cotangent)


def dot_t(a, b):
    return lax.dot_general(a, b, (((1,), (1,)), ((), ())), preferred_element_type=F32)


def expert_kernel(
    arr_hbm, wu_hbm, wd_hbm, send_hbm, x_hbm, c_hbm, hid_hbm, gp_hbm,
    arr_ref, wu_ref, wd_ref, send_ref, perm, rows, back_rows, hid, gp, load_sem, store_sem,
):
    m, half = arr_ref.shape
    n = m // 4
    part = n // 2
    block = m // 2
    halves = [pl.ds(a * block, block) for a in range(2)]
    loads = [(arr_hbm.at[here, :], arr_ref.at[here, :]) for here in halves]
    loads += [(wu_hbm.at[pl.ds(h * half, half), :], wu_ref.at[pl.ds(h * half, half), :]) for h in range(2)]
    loads += [(wd_hbm, wd_ref)]
    loads = [pltpu.make_async_copy(src, dst, load_sem.at[i]) for i, (src, dst) in enumerate(loads)]
    for copy in loads:
        copy.start()
    t = iota((part, block), 0)
    at = (t // 2) * 8 + t % 2
    for b in range(4):
        perm[pl.ds(b * part, part), :] = one_hot(iota((part, block), 1) == at + 2 * b)
    for a in range(2):
        loads[a].wait()
        moved = jnp.dot(perm[...], arr_ref[pl.ds(a * block, block), :], preferred_element_type=F32).astype(BF16)
        for b in range(4):
            rows[pl.ds(b * n + a * part, part), :] = moved[b * part : (b + 1) * part]
    stores = []

    def store(src, dst):
        copy = pltpu.make_async_copy(src, dst, store_sem.at[len(stores)])
        copy.start()
        stores.append(copy)

    for h in range(2):
        cols = pl.ds(h * half, half)
        store(rows.at[pl.ds(h * n, n), :], x_hbm.at[:, cols])
        store(rows.at[pl.ds((2 + h) * n, n), :], c_hbm.at[:, cols])
    pre = jnp.zeros((n, wu_ref.shape[1]), F32)
    for h in range(2):
        loads[2 + h].wait()
        pre += jnp.dot(rows[pl.ds(h * n, n), :], wu_ref[pl.ds(h * half, half), :], preferred_element_type=F32)
    sigma = 1.0 / (1.0 + jnp.exp(-pre))
    hidden = (pre * sigma).astype(BF16)
    hid[...] = hidden
    store(hid, hid_hbm)
    loads[4].wait()
    back = jnp.zeros((n, wu_ref.shape[1]), F32)
    for h in range(2):
        back += dot_t(rows[pl.ds((2 + h) * n, n), :], wd_ref[:, pl.ds(h * half, half)])
    grad = (back * sigma * (1.0 + pre * (1.0 - sigma))).astype(BF16)
    gp[...] = grad
    store(gp, gp_hbm)
    for h in range(2):
        cols = pl.ds(h * half, half)
        out = jnp.dot(hidden, wd_ref[:, cols], preferred_element_type=F32).astype(BF16)
        xgrad = dot_t(grad, wu_ref[cols, :]).astype(BF16)
        for a in range(2):
            took = slice(a * part, (a + 1) * part)
            back_rows[pl.ds(a * block + h * part, part), :] = out[took]
            back_rows[pl.ds(a * block + (2 + h) * part, part), :] = xgrad[took]
    for a in range(2):
        here = pl.ds(a * block, block)
        send_ref[here, :] = lax.dot_general(
            perm[...], back_rows[here, :], (((0,), (0,)), ((), ())), preferred_element_type=F32
        ).astype(BF16)
        store(send_ref.at[here, :], send_hbm.at[here, :])
    for copy in stores:
        copy.wait()


def expert(arrived, w_up, w_down):
    m, half = arrived.shape
    n, width, ff = m // 4, 2 * half, w_up.shape[1]
    shape = jax.ShapeDtypeStruct
    return pl.pallas_call(
        expert_kernel,
        out_shape=(
            shape((m, half), BF16),
            shape((n, width), BF16),
            shape((n, width), BF16),
            shape((n, ff), BF16),
            shape((n, ff), BF16),
        ),
        in_specs=[IN_HBM] * 3,
        out_specs=[IN_HBM] * 5,
        scratch_shapes=[
            pltpu.VMEM((m, half), BF16),
            pltpu.VMEM((width, ff), BF16),
            pltpu.VMEM((ff, width), BF16),
            pltpu.VMEM((m, half), BF16),
            pltpu.VMEM((m // 2, m // 2), BF16),
            pltpu.VMEM((m, half), BF16),
            pltpu.VMEM((m, half), BF16),
            pltpu.VMEM((n, ff), BF16),
            pltpu.VMEM((n, ff), BF16),
            pltpu.SemaphoreType.DMA((5,)),
            pltpu.SemaphoreType.DMA((8,)),
        ],
        compiler_params=pltpu.CompilerParams(vmem_limit_bytes=VMEM_LIMIT),
        name="expert",
    )(arrived, w_up, w_down)


def plan_kernel(ids_ref, place_ref, after_ref, sel):
    m = sel.shape[0]
    n = m // 4
    base = column(row_base(ids_ref[...], place_ref)).astype(I32)[:, :1]
    cols = iota((n, m), 1)
    for b in range(4):
        sel[pl.ds(b * n, n), :] = one_hot(cols == base + 2 * b)


def plan(ids, place, after):
    m = 4 * ids.shape[1]
    return pl.pallas_call(
        plan_kernel,
        out_shape=jax.ShapeDtypeStruct((m, m), BF16),
        in_specs=[ON_CHIP, ON_CHIP, IN_HBM],
        out_specs=ON_CHIP,
        name="plan",
    )(ids, place, after)


def combine_kernel(sel_ref, gate_ref, arr_ref, out_ref, grad_ref):
    n = out_ref.shape[0]
    h = pl.program_id(0)
    gate = column(gate_ref[...])[:, :1]
    o = jnp.dot(sel_ref[pl.ds(h * n, n), :], arr_ref[...], preferred_element_type=F32)
    g = jnp.dot(sel_ref[pl.ds((2 + h) * n, n), :], arr_ref[...], preferred_element_type=F32)
    out_ref[...] = (gate * o).astype(BF16)
    grad_ref[...] = g.astype(BF16)


def combine(sel, gate, arrived, n, width):
    shape = jax.ShapeDtypeStruct((n, width), BF16)
    block = pl.BlockSpec((n, width // 2), lambda h: (0, h))
    return pl.pallas_call(
        combine_kernel,
        out_shape=(shape, shape),
        grid=(2,),
        in_specs=[ON_CHIP] * 3,
        out_specs=[block, block],
        compiler_params=pltpu.CompilerParams(vmem_limit_bytes=VMEM_LIMIT // 3),
        name="combine",
    )(sel, gate, arrived)


def wgrad_kernel(where_ref, x_ref, c_ref, hid_ref, gp_ref, up_ref, down_ref, hid_t, side):
    i = pl.program_id(0)

    @pl.when(i == 0)
    def _():
        hid_t[...] = hid_ref[...].T

    block = up_ref.shape[1]
    numbers = (((0,), (0,)), ((), ()))

    def columns(px, py):
        return pl.ds(pl.multiple_of((lax.rem(px, side) * side + lax.rem(py, side)) * block, block), block)

    for k in range(side):
        x = x_ref[:, columns(where_ref[0] + i, where_ref[1] + k)]
        c = c_ref[:, columns(where_ref[0] + k, where_ref[1] + i)]
        up_ref[k] = lax.dot_general(x, gp_ref[...], numbers, preferred_element_type=F32).astype(BF16)
        down_ref[k] = jnp.dot(hid_t[...], c, preferred_element_type=F32).astype(BF16)


def wgrad(where, rows_x, rows_c, hidden, grad, side):
    n, width = rows_x.shape
    ff = hidden.shape[1]
    parts = side * side
    block = width // parts
    whole = lambda i, where: (0, 0)
    at = lambda i, where: (i, 0, 0)
    return pl.pallas_call(
        functools.partial(wgrad_kernel, side=side),
        grid_spec=pltpu.PrefetchScalarGridSpec(
            num_scalar_prefetch=1,
            grid=(side,),
            in_specs=[
                pl.BlockSpec((n, width), whole),
                pl.BlockSpec((n, width), whole),
                pl.BlockSpec((n, ff), whole),
                pl.BlockSpec((n, ff), whole),
            ],
            out_specs=[pl.BlockSpec((side, block, ff), at), pl.BlockSpec((side, ff, block), at)],
            scratch_shapes=[pltpu.VMEM((ff, n), BF16)],
        ),
        out_shape=(
            jax.ShapeDtypeStruct((parts, block, ff), BF16),
            jax.ShapeDtypeStruct((parts, ff, block), BF16),
        ),
        cost_estimate=pl.CostEstimate(
            flops=4 * n * width * ff, bytes_accessed=4 * width * ff + 4 * n * (width + ff), transcendentals=0
        ),
        name="wgrad",
    )(where, rows_x, rows_c, hidden, grad)


def ring_scatter(a, axis, side, last):
    def send(v, step):
        pairs = []
        for px in range(side):
            for py in range(side):
                tx, ty = ((px + step) % side, py) if axis == "x" else (px, (py + step) % side)
                pairs.append((px * side + py, tx * side + ty))
        return lax.ppermute(v, "dp", pairs)

    half = a.shape[1] // 2
    add = lambda p, q: (p.astype(F32) + q.astype(F32)).astype(BF16)
    ahead = send(a[2, :half], 1)
    behind = send(a[2, half:], -1)
    ahead = send(jnp.concatenate([add(a[1, :half], ahead), a[1, half:]], 0), 1)
    behind = send(jnp.concatenate([a[3, :half], add(a[3, half:], behind)], 0), -1)
    total = a[0].astype(F32) + ahead.astype(F32) + behind.astype(F32)
    return total * (1.0 / (side * side)) if last else total.astype(BF16)


def scatter(parts, order, side):
    count, rows, cols = parts.shape
    first = ring_scatter(parts.reshape(side, side * rows, cols), order[0], side, False)
    return ring_scatter(first.reshape(side, rows, cols), order[1], side, True)


CHIP_ORDER = (19, 6, 9, 20, 24, 22, 27, 1, 10, 28, 3, 13, 2, 5, 18, 25,
              23, 17, 7, 14, 31, 15, 26, 0, 12, 4, 11, 29, 16, 21, 8, 30)


def exchange_order(experts):
    return [2 * chip + core for chip in CHIP_ORDER for core in range(2)]


def shards(tokens, expert_ids, gate, cotangent, w_up, w_down):
    n, width = tokens.shape
    experts = lax.axis_size("expert")
    order = exchange_order(experts)
    side = 4
    ids = expert_ids.reshape(1, n)
    gates = gate.reshape(1, n)

    def exchange(v):
        v = v.reshape(experts, -1, v.shape[1])
        v = lax.all_to_all(
            v, "expert", split_axis=0, concat_axis=0, tiled=True, axis_index_groups=[order]
        )
        return v.reshape(-1, v.shape[2])

    place = np.zeros((experts, n), np.float32)
    place[order] = np.arange(experts)[:, None]
    arrived = exchange(dispatch(ids, place, gates, tokens, cotangent))
    send, rows_x, rows_c, hidden, grad = expert(arrived, w_up[0], w_down[0])
    returned = exchange(send)
    here = lax.axis_index("dp")
    where = jnp.stack([here // side, here % side]).astype(I32)
    up, down = wgrad(where, rows_x, rows_c, hidden, grad, side)
    up = scatter(up, "xy", side)
    down = scatter(down, "yx", side)
    layer_out, token_grad = combine(plan(ids, place, grad), gates, returned, n, width)
    return layer_out, token_grad, up[None], down[None]


def solution(mesh):
    in_specs = (
        P(("dp", "expert"), None),
        P(("dp", "expert")),
        P(("dp", "expert")),
        P(("dp", "expert"), None),
        P("expert", None, None),
        P("expert", None, None),
    )
    out_specs = (
        P(("dp", "expert"), None),
        P(("dp", "expert"), None),
        P("expert", "dp", None),
        P("expert", None, "dp"),
    )
    return jax.shard_map(shards, mesh=mesh, in_specs=in_specs, out_specs=out_specs, check_vma=False)
```
